1024 devices in a mesh: wide: 16 (over x, y_hi, core), narrow: 64 (over z, y_lo).
Axes of the slice: x: 4, y: 4 (y_hi: 2, y_lo: 2; y = y_hi * 2 + y_lo), z: 32, core: 2. Of those that a mesh axis runs over, the one named last changes fastest.
Arguments:
- state: float32 [2, 33554432], P(None, ('wide', 'narrow')), may hold values from -6 to 6
- gates: float32 [6, 2, 128, 128], replicated, may hold values from -0.375 to 0.375
Outputs:
- amplitudes: float32 [2, 33554432], P(None, ('wide', 'narrow'))
The draws below stay inside these ranges and needn't reach their ends.
All inputs are finite; a program needn't handle non-finite values.
Results may differ from the reference program's by a relative error of at most 0.0001.
Values sent between devices are 32-bit elements; how exact they have to be, the bound alone decides.
A program may use at most 32 MiB of HBM per device.

```python
import jax
import jax.numpy as jnp
from jax import lax

GATE_DIM = 128
LAYERS = 3
GATES = 6
AMPS = 33554432
N_WIDE = 16
N_NARROW = 64


def levels(rng, dims, shards, smallest, largest):
    level = 1.0
    for dim, parts in shards:
        heights = jax.random.uniform(jax.random.fold_in(jax.random.fold_in(rng, 6), dim), (parts,), jnp.float32, smallest / len(shards), largest / len(shards))
        level = level * jnp.repeat(jnp.exp(heights), dims[dim] // parts).reshape((-1,) + (1,) * (len(dims) - 1 - dim))
    return level


def scatter_about(key, shape, width, reach, split=(), kind=jnp.bfloat16):
    drawn = jax.random.normal(key, shape, jnp.float32) * width
    if len(split) > 0:
        drawn = levels(key, shape, split, -0.22, 0.18) * drawn
    return jnp.clip(drawn, min=-reach, max=reach).astype(kind)


def setup_inputs(seed: int = 0) -> dict:
    key_of = jax.random.split(jax.random.key(seed), 3)
    return {
        "state": scatter_about(key_of[0], (2, AMPS), 1.0, 6.0, ((1, 1024),), jnp.float32),
        "gates": scatter_about(key_of[1], (GATES, 2, GATE_DIM, GATE_DIM), (2 * GATE_DIM) ** -0.5, 0.375, (), jnp.float32),
    }


def gate_all(flat_state, joined_gate):
    gate_dim = joined_gate.shape[-1]
    block_count = flat_state.shape[1]
    columns = flat_state.shape[2] // gate_dim
    shaped = flat_state.reshape(2, block_count, gate_dim, columns)
    matrix = jnp.stack([jnp.stack([joined_gate[0], -joined_gate[1]]), jnp.stack([joined_gate[1], joined_gate[0]])])
    result = jnp.einsum("cdir,kcji->kdrj", shaped, matrix, precision=lax.Precision.HIGHEST)
    return result.reshape(2, block_count, columns * gate_dim)


def reference(state, gates):
    block_count = N_WIDE * N_NARROW
    per_block = state.shape[1] // block_count
    rest_count = per_block // block_count
    flat_state = state.reshape(2, block_count, per_block)
    for layer_index in range(LAYERS):
        flat_state = gate_all(flat_state, gates[2 * layer_index])
        flat_state = gate_all(flat_state, gates[2 * layer_index + 1])
        if layer_index + 1 < LAYERS:
            shaped = flat_state.reshape(2, N_WIDE, N_NARROW, N_WIDE, N_NARROW, rest_count)
            flat_state = shaped.transpose(0, 3, 4, 1, 2, 5).reshape(2, block_count, per_block)
    return flat_state.reshape(2, block_count * per_block)
```

```python
import jax
import jax.numpy as jnp
from jax import lax
from jax.sharding import PartitionSpec as P

AXES = ("wide", "narrow")


def apply_layer(x, u, v):
    um = jnp.stack([jnp.stack([u[0], -u[1]]), jnp.stack([u[1], u[0]])])
    vm = jnp.stack([jnp.stack([v[0], -v[1]]), jnp.stack([v[1], v[0]])])
    y = jnp.einsum("kcji,ciqs->ksjq", um, x, precision=lax.Precision.HIGHEST)
    return jnp.einsum("ksjq,mkpq->msjp", y, vm, precision=lax.Precision.HIGHEST)


def remap(x):
    blocks = lax.axis_size("wide") * lax.axis_size("narrow")
    shaped = x.reshape(2, blocks, -1).transpose(1, 0, 2)
    moved = lax.all_to_all(shaped, AXES, split_axis=0, concat_axis=0, tiled=True)
    return moved.transpose(1, 0, 2).reshape(2, -1)


def on_device(state, gates):
    x = state
    layers = gates.shape[0] // 2
    dim = gates.shape[-1]
    for l in range(layers):
        y = apply_layer(x.reshape(2, dim, dim, -1), gates[2 * l], gates[2 * l + 1])
        x = y.reshape(2, -1)
        if l + 1 < layers:
            x = remap(x)
    return x


def solution(mesh):
    return jax.shard_map(
        on_device,
        mesh=mesh,
        in_specs=(P(None, AXES), P()),
        out_specs=P(None, AXES),
        check_vma=False,
    )
```

```python
import jax
import jax.numpy as jnp
from jax import lax
from jax.experimental import pallas as pl
from jax.experimental.pallas import tpu as pltpu
from jax.sharding import PartitionSpec as P

AXES = ("wide", "narrow")
MESH = pl.DeviceIdType.MESH
NZ = 32
NP = 32


def dot(a, b):
    return lax.dot_general(
        a, b, (((1,), (0,)), ((), ())), precision=lax.Precision.HIGHEST, preferred_element_type=jnp.float32
    )


def dot_nt(a, b):
    return lax.dot_general(
        a, b, (((1,), (1,)), ((), ())), precision=lax.Precision.HIGHEST, preferred_element_type=jnp.float32
    )


def iota(shape, dim):
    return lax.broadcasted_iota(jnp.int32, shape, dim)


def in_parts(k, first):
    if first:
        return (k >> 8) * 64 + ((k >> 1) & 63), k & 1, (k >> 7) & 1
    return (k >> 6) * 16 + ((k >> 1) & 15), k & 1, (k >> 5) & 1


def out_parts(k, last):
    if last:
        return k & 127, (k >> 7) & 1, k >> 8
    return ((k >> 6) & 1) * 64 + ((k >> 7) & 1) * 32 + (k & 31), k >> 8, (k >> 5) & 1


def expand_second(u, first, last):
    i2, _, _ = in_parts(iota((512, 128), 0), first)
    rows = (i2 == iota((512, 128), 1)).astype(jnp.float32)
    j2, _, _ = out_parts(iota((128, 512), 1), last)
    cols = (j2 == iota((128, 512), 0)).astype(jnp.float32)
    real = dot(dot_nt(rows, u[:128]), cols)
    imag = dot(dot_nt(rows, u[128:]), cols)
    _, s_in, c_in = in_parts(iota((512, 512), 0), first)
    _, s_out, c_out = out_parts(iota((512, 512), 1), last)
    full = jnp.where(c_in == c_out, real, jnp.where(c_in < c_out, imag, -imag))
    return jnp.where(s_in == s_out, full, 0.0)


def permute_first(u):
    k = iota((128, 128), 1)
    pick = (iota((128, 128), 0) == (k & 15) * 8 + (k >> 4)).astype(jnp.float32)
    return dot(u, pick)


def times_i(tiles, first, roll):
    if first:
        return [-tiles[1], tiles[0], -tiles[3], tiles[2]]
    real = ((iota((128, 128), 1) >> 5) & 1) == 0
    return [jnp.where(real, -roll(t, 96), roll(t, 32)) for t in tiles]


def layer(tiles, u1, m, first, roll):
    both = [dot(u1, t) for t in tiles]
    turned = times_i([t[128:] for t in both], first, roll)
    z = jnp.concatenate([a[:128] + b for a, b in zip(both, turned)], axis=1)
    return dot(z, m)


def lane_roll(x, by):
    return pltpu.roll(x, by, 1)


def kernel(state, gates, out, s1, r1, s2, r2, mats, firsts, plane_send, plane_recv, z_send, z_recv):
    wide = lax.axis_index("wide")
    narrow = lax.axis_index("narrow")
    z = narrow // 2
    plane = (wide // 8) * 16 + (narrow % 2) * 8 + wide % 8

    def plane_id(p):
        return ((p // 16) * 8 + p % 8, z * 2 + (p // 8) % 2)

    def z_id(other):
        return (wide, other * 2 + narrow % 2)

    def z_slot(other):
        return (other % 4) * 8 + other // 4

    barrier = pltpu.get_barrier_semaphore()

    def greet(k, _):
        pl.semaphore_signal(barrier, inc=1, device_id=z_id((z + k) % NZ), device_id_type=MESH)
        pl.semaphore_signal(barrier, inc=1, device_id=plane_id((plane + k) % NP), device_id_type=MESH)
        return 0

    lax.fori_loop(1, 32, greet, 0)

    def send_plane(o, t):
        for part in range(4):
            s1[t, part * 8 : part * 8 + 8] = o[:, part * 128 : part * 128 + 128].reshape(8, 16, 128)

    def start_plane(t):
        pltpu.make_async_copy(s1.at[t, plane], r1.at[t, plane], plane_recv.at[t]).start()

        def send(k, _):
            p = (plane + k) % NP
            pltpu.make_async_remote_copy(
                src_ref=s1.at[t, p],
                dst_ref=r1.at[t, plane],
                send_sem=plane_send.at[t],
                recv_sem=plane_recv.at[t],
                device_id=plane_id(p),
                device_id_type=MESH,
            ).start()
            return 0

        lax.fori_loop(1, NP, send, 0)

    def wait_plane(t):
        pltpu.make_async_copy(r1.at[t], r1.at[t], plane_recv.at[t]).wait()

    def shuffle(t):
        low = iota((16, 128), 1) < 64
        for w in range(16):
            p = (w // 8) * 16 + w % 8
            a = r1[t, p]
            b = r1[t, p + 8]
            s2[t, pl.ds(w, 16, 32), :] = jnp.where(low, a, lane_roll(b, 64))
            s2[t, pl.ds(16 + w, 16, 32), :] = jnp.where(low, lane_roll(a, 64), b)

    def start_z(t):
        def copy(other):
            return pltpu.make_async_remote_copy(
                src_ref=s2.at[t, pl.ds(pl.multiple_of(other * 16, 16), 16)],
                dst_ref=r2.at[t, z_slot(z)],
                send_sem=z_send.at[t],
                recv_sem=z_recv.at[t],
                device_id=z_id(other),
                device_id_type=MESH,
            )

        copy((z + 16) % NZ).start()

        def send(k, _):
            copy((z + 16 - k) % NZ).start()
            copy((z + 16 + k) % NZ).start()
            return 0

        lax.fori_loop(1, 16, send, 0)
        pltpu.make_async_copy(
            s2.at[t, pl.ds(pl.multiple_of(z * 16, 16), 16)], r2.at[t, z_slot(z)], z_recv.at[t]
        ).start()

    def wait_z(t):
        pltpu.make_async_copy(r2.at[t], r2.at[t], z_recv.at[t]).wait()

    def prepare(l):
        mats[l] = expand_second(gates[2 * l + 1], l == 0, l == 2)
        if l > 0:
            firsts[l - 1] = permute_first(gates[2 * l])

    prepare(0)
    tiles = [state[pl.ds(q, 128, 4), :] for q in range(4)]
    o = layer(tiles, gates[0], mats[0], True, lane_roll)
    for l in range(1, 3):
        t = l - 1
        send_plane(o, t)
        if l == 1:
            pl.semaphore_wait(barrier, 62)
        start_plane(t)
        wait_plane(t)
        shuffle(t)
        start_z(t)
        prepare(l)
        wait_z(t)
        tiles = [r2[t, q * 8 : q * 8 + 8].reshape(128, 128) for q in range(4)]
        o = layer(tiles, firsts[t], mats[l], False, lane_roll)
    for c in range(2):
        for s in range(2):
            q = c * 2 + s
            out[pl.ds(s * 256 + c, 128, 2), :] = o[:, q * 128 : q * 128 + 128]
    for t in range(2):
        pltpu.make_async_copy(s1.at[t, pl.ds(0, 31)], s1.at[t, pl.ds(0, 31)], plane_send.at[t]).wait()
        pltpu.make_async_copy(s2.at[t, pl.ds(0, 496)], s2.at[t, pl.ds(0, 496)], z_send.at[t]).wait()


def on_device(state, gates):
    rows = state.reshape(2, 256, 128).transpose(1, 0, 2).reshape(512, 128)
    vmem = pl.BlockSpec(memory_space=pltpu.VMEM)
    out = pl.pallas_call(
        kernel,
        out_shape=jax.ShapeDtypeStruct((512, 128), jnp.float32),
        in_specs=[vmem, vmem],
        out_specs=vmem,
        scratch_shapes=[
            pltpu.VMEM((2, NP, 16, 128), jnp.float32),
            pltpu.VMEM((2, NP, 16, 128), jnp.float32),
            pltpu.VMEM((2, NZ * 16, 128), jnp.float32),
            pltpu.VMEM((2, NZ, 16, 128), jnp.float32),
            pltpu.VMEM((3, 512, 512), jnp.float32),
            pltpu.VMEM((2, 256, 128), jnp.float32),
            pltpu.SemaphoreType.DMA((2,)),
            pltpu.SemaphoreType.DMA((2,)),
            pltpu.SemaphoreType.DMA((2,)),
            pltpu.SemaphoreType.DMA((2,)),
        ],
        compiler_params=pltpu.CompilerParams(collective_id=0, has_side_effects=True),
        name="window",
    )(rows, gates.reshape(6, 256, 128))
    return out.reshape(256, 2, 128).transpose(1, 0, 2).reshape(2, 32768)


def solution(mesh):
    return jax.shard_map(
        on_device,
        mesh=mesh,
        in_specs=(P(None, AXES), P()),
        out_specs=P(None, AXES),
        check_vma=False,
    )
```

```python
import jax
import jax.numpy as jnp
from jax import lax
from jax.experimental import pallas as pl
from jax.experimental.pallas import tpu as pltpu
from jax.sharding import PartitionSpec as P

AXES = ("wide", "narrow")
MESH = pl.DeviceIdType.MESH
NZ = 32
NP = 32


def dot(a, b):
    return lax.dot_general(
        a, b, (((1,), (0,)), ((), ())), precision=lax.Precision.HIGHEST, preferred_element_type=jnp.float32
    )


def dot_nt(a, b):
    return lax.dot_general(
        a, b, (((1,), (1,)), ((), ())), precision=lax.Precision.HIGHEST, preferred_element_type=jnp.float32
    )


def iota(shape, dim):
    return lax.broadcasted_iota(jnp.int32, shape, dim)


def in_parts(k, first):
    if first:
        return (k >> 8) * 64 + ((k >> 1) & 63), k & 1, (k >> 7) & 1
    return (k >> 6) * 16 + ((k >> 1) & 15), k & 1, (k >> 5) & 1


def out_parts(k, last):
    if last:
        return k & 127, (k >> 7) & 1, k >> 8
    return ((k >> 6) & 1) * 64 + ((k >> 7) & 1) * 32 + (k & 31), k >> 8, (k >> 5) & 1


def expand_second(u, first, last):
    i2, _, _ = in_parts(iota((512, 128), 0), first)
    rows = (i2 == iota((512, 128), 1)).astype(jnp.float32)
    j2, _, _ = out_parts(iota((128, 512), 1), last)
    cols = (j2 == iota((128, 512), 0)).astype(jnp.float32)
    real = dot(dot_nt(rows, u[:128]), cols)
    imag = dot(dot_nt(rows, u[128:]), cols)
    _, s_in, c_in = in_parts(iota((512, 512), 0), first)
    _, s_out, c_out = out_parts(iota((512, 512), 1), last)
    full = jnp.where(c_in == c_out, real, jnp.where(c_in < c_out, imag, -imag))
    return jnp.where(s_in == s_out, full, 0.0)


def permute_first(u):
    k = iota((128, 128), 1)
    pick = (iota((128, 128), 0) == (k & 15) * 8 + (k >> 4)).astype(jnp.float32)
    return dot(u, pick)


def times_i(tiles, first, roll):
    if first:
        return [-tiles[1], tiles[0], -tiles[3], tiles[2]]
    real = ((iota((128, 128), 1) >> 5) & 1) == 0
    return [jnp.where(real, -roll(t, 96), roll(t, 32)) for t in tiles]


def layer(tiles, u1, m, first, roll):
    both = [dot(u1, t) for t in tiles]
    turned = times_i([t[128:] for t in both], first, roll)
    z = jnp.concatenate([a[:128] + b for a, b in zip(both, turned)], axis=1)
    return dot(z, m)


def lane_roll(x, by):
    return pltpu.roll(x, by, 1)


def kernel(state_hbm, gates_hbm, out, state, gates, s1, r1, s2, r2, mats, firsts, *sems):
    load, plane_send, plane_recv, z_send, z_recv, relay = sems
    wide = lax.axis_index("wide")
    narrow = lax.axis_index("narrow")
    z = narrow // 2
    mine = z // 16
    plane = (wide // 8) * 16 + (narrow % 2) * 8 + wide % 8

    def plane_id(p):
        return ((p // 16) * 8 + p % 8, z * 2 + (p // 8) % 2)

    def z_id(other):
        return (wide, other * 2 + narrow % 2)

    def z_slot(other):
        return (other % 4) * 8 + other // 4

    def signal_z(sem, step):
        for other in ((z + step) % NZ, (z + NZ - step) % NZ):
            pl.semaphore_signal(sem, inc=1, device_id=z_id(other), device_id_type=MESH)

    barrier = pltpu.get_barrier_semaphore()

    def greet(k, _):
        pl.semaphore_signal(barrier, inc=1, device_id=plane_id((plane + k) % NP), device_id_type=MESH)
        return 0

    signal_z(barrier, 1)
    lax.fori_loop(1, NP, greet, 0)
    loads = [
        pltpu.make_async_copy(gates_hbm.at[pl.ds(0, 2)], gates.at[pl.ds(0, 2)], load.at[0]),
        pltpu.make_async_copy(state_hbm, state, load.at[1]),
        pltpu.make_async_copy(gates_hbm.at[pl.ds(2, 4)], gates.at[pl.ds(2, 4)], load.at[2]),
    ]
    for copy in loads:
        copy.start()

    def half(phase):
        return 1 - mine if phase == 0 else mine

    def place(o, t):
        for part in range(4):
            tile = o[:, part * 128 : part * 128 + 128].reshape(8, 2, 8, 128)
            for h in range(2):
                s1[t, h, part * 8 : part * 8 + 8] = tile[:, h]

    def start_plane(t, phase):
        h = half(phase)
        pltpu.make_async_copy(s1.at[t, h, plane], r1.at[t, h, plane], plane_recv.at[t, phase]).start()

        def send(k, _):
            p = (plane + k) % NP
            pltpu.make_async_remote_copy(
                src_ref=s1.at[t, h, p],
                dst_ref=r1.at[t, h, plane],
                send_sem=plane_send.at[t],
                recv_sem=plane_recv.at[t, phase],
                device_id=plane_id(p),
                device_id_type=MESH,
            ).start()
            return 0

        lax.fori_loop(1, NP, send, 0)

    def wait_plane(t, phase):
        h = half(phase)
        pltpu.make_async_copy(r1.at[t, h], r1.at[t, h], plane_recv.at[t, phase]).wait()

    def shuffle(t, phase):
        h = half(phase)
        low = iota((8, 128), 1) < 64
        for w in range(16):
            p = (w // 8) * 16 + w % 8
            a = r1[t, h, p]
            b = r1[t, h, p + 8]
            s2[t, h, pl.ds(w, 8, 32), :] = jnp.where(low, a, lane_roll(b, 64))
            s2[t, h, pl.ds(16 + w, 8, 32), :] = jnp.where(low, lane_roll(a, 64), b)

    def start_z(t, phase):
        h = half(phase)

        def block(j):
            return s2.at[t, h, pl.ds(pl.multiple_of(j * 16, 16), 16)]

        def send(k, _):
            j = (z + k) % 16
            pltpu.make_async_remote_copy(
                src_ref=block(j),
                dst_ref=r2.at[t, z_slot(z)],
                send_sem=z_send.at[t],
                recv_sem=z_recv.at[t],
                device_id=z_id(h * 16 + j),
                device_id_type=MESH,
            ).start()
            return 0

        if phase == 0:
            send(0, 0)
        else:
            pltpu.make_async_copy(block(z % 16), r2.at[t, z_slot(z)], z_recv.at[t]).start()

        def pair(k, _):
            send(k, 0)
            return send(16 - k, 0)

        lax.fori_loop(1, 8, pair, 0)
        send(8, 0)

    def wait_z(t):
        pltpu.make_async_copy(r2.at[t], r2.at[t], z_recv.at[t]).wait()

    def prepare(l):
        mats[l] = expand_second(gates[2 * l + 1], l == 0, l == 2)
        if l > 0:
            firsts[l - 1] = permute_first(gates[2 * l])

    loads[0].wait()
    prepare(0)
    pl.semaphore_wait(barrier, 33)
    signal_z(relay.at[0], 1)
    loads[1].wait()
    loads[2].wait()
    tiles = [state[pl.ds(q, 128, 4), :] for q in range(4)]
    o = layer(tiles, gates[0], mats[0], True, lane_roll)
    for l in range(1, 3):
        t = l - 1
        place(o, t)
        start_plane(t, 0)
        start_plane(t, 1)
        if l == 1:
            for step in range(4):
                pl.semaphore_wait(relay.at[step], 2)
                if step < 3:
                    signal_z(relay.at[step + 1], 2 << step)
        for phase in range(2):
            wait_plane(t, phase)
            shuffle(t, phase)
            start_z(t, phase)
        prepare(l)
        wait_z(t)
        tiles = [r2[t, q * 8 : q * 8 + 8].reshape(128, 128) for q in range(4)]
        o = layer(tiles, firsts[t], mats[l], False, lane_roll)
    for c in range(2):
        for s in range(2):
            q = c * 2 + s
            out[pl.ds(s * 256 + c, 128, 2), :] = o[:, q * 128 : q * 128 + 128]
    done = s2.at[0, :, pl.ds(0, 248)]
    for t in range(2):
        for sem in (plane_send, z_send):
            pltpu.make_async_copy(done, done, sem.at[t]).wait()


def on_device(state, gates):
    rows = state.reshape(2, 256, 128).transpose(1, 0, 2).reshape(512, 128)
    hbm = pl.BlockSpec(memory_space=pl.ANY)
    out = pl.pallas_call(
        kernel,
        out_shape=pltpu.VMEM((512, 128), jnp.float32),
        in_specs=[hbm, hbm],
        out_specs=pl.BlockSpec(memory_space=pltpu.VMEM),
        scratch_shapes=[
            pltpu.VMEM((512, 128), jnp.float32),
            pltpu.VMEM((6, 256, 128), jnp.float32),
            pltpu.VMEM((2, 2, NP, 8, 128), jnp.float32),
            pltpu.VMEM((2, 2, NP, 8, 128), jnp.float32),
            pltpu.VMEM((2, 2, NZ * 8, 128), jnp.float32),
            pltpu.VMEM((2, NZ, 16, 128), jnp.float32),
            pltpu.VMEM((3, 512, 512), jnp.float32),
            pltpu.VMEM((2, 256, 128), jnp.float32),
            pltpu.SemaphoreType.DMA((3,)),
            pltpu.SemaphoreType.DMA((2,)),
            pltpu.SemaphoreType.DMA((2, 2)),
            pltpu.SemaphoreType.DMA((2,)),
            pltpu.SemaphoreType.DMA((2,)),
            pltpu.SemaphoreType.REGULAR((4,)),
        ],
        compiler_params=pltpu.CompilerParams(collective_id=0, has_side_effects=True),
        name="window",
    )(rows, gates.reshape(6, 256, 128))
    return out.reshape(256, 2, 128).transpose(1, 0, 2).reshape(2, 32768)


def solution(mesh):
    return jax.shard_map(
        on_device,
        mesh=mesh,
        in_specs=(P(None, AXES), P()),
        out_specs=P(None, AXES),
        check_vma=False,
    )
```

```python
import jax
import jax.numpy as jnp
from jax import lax
from jax.experimental import pallas as pl
from jax.experimental.pallas import tpu as pltpu
from jax.sharding import PartitionSpec as P

AXES = ("wide", "narrow")
MESH = pl.DeviceIdType.MESH
NZ = 32
NP = 32


def dot(a, b):
    return lax.dot_general(
        a, b, (((1,), (0,)), ((), ())), precision=lax.Precision.HIGHEST, preferred_element_type=jnp.float32
    )


def dot_nt(a, b):
    return lax.dot_general(
        a, b, (((1,), (1,)), ((), ())), precision=lax.Precision.HIGHEST, preferred_element_type=jnp.float32
    )


def iota(shape, dim):
    return lax.broadcasted_iota(jnp.int32, shape, dim)


def in_parts(k, l):
    if l == 0:
        return (k >> 8) * 64 + ((k >> 1) & 63), k & 1, (k >> 7) & 1
    if l == 1:
        return ((k >> 6) & 1) * 64 + (k >> 7) * 32 + ((k >> 5) & 1) * 16 + (k & 15), 0 * k, (k >> 4) & 1
    return (k >> 6) * 16 + ((k >> 1) & 15), k & 1, (k >> 5) & 1


def out_parts(k, l):
    if l == 0:
        high = ((k >> 5) & 1) * 64 + ((k >> 6) & 1) * 32
        return high + (k & 15) * 2 + ((k >> 7) & 1), k >> 8, (k >> 4) & 1
    if l == 1:
        return ((k >> 6) & 1) * 64 + (k >> 7) * 32 + (k & 31), 0 * k, (k >> 5) & 1
    return k & 127, (k >> 7) & 1, k >> 8


def select_second(u, l, n):
    i2, _, _ = in_parts(iota((n, 128), 0), l)
    rows = (i2 == iota((n, 128), 1)).astype(jnp.float32)
    j2, _, _ = out_parts(iota((128, n), 1), l)
    cols = (j2 == iota((128, n), 0)).astype(jnp.float32)
    return dot(dot_nt(rows, u[:128]), cols), dot(dot_nt(rows, u[128:]), cols)


def join_second(real, imag, l, n):
    _, s_in, c_in = in_parts(iota((n, n), 0), l)
    _, s_out, c_out = out_parts(iota((n, n), 1), l)
    full = jnp.where(c_in == c_out, real, jnp.where(c_in < c_out, imag, -imag))
    return jnp.where(s_in == s_out, full, 0.0)


def expand_second(u, l, n):
    return join_second(*select_second(u, l, n), l, n)


def permute_first(u):
    k = iota((128, 128), 1)
    pick = (iota((128, 128), 0) == (k & 15) * 8 + (k >> 4)).astype(jnp.float32)
    return dot(u, pick)


def times_i(tiles, l, roll):
    if l == 0:
        return [-tiles[1], tiles[0], -tiles[3], tiles[2]]
    step = 16 if l == 1 else 32
    real = (iota((128, 128), 1) & step) == 0
    return [jnp.where(real, -roll(t, 128 - step), roll(t, step)) for t in tiles]


def first_gate(tiles, u1, l, roll):
    both = [dot(u1, t) for t in tiles]
    turned = times_i([t[128:] for t in both], l, roll)
    return jnp.concatenate([a[:128] + b for a, b in zip(both, turned)], axis=1)


def swap_half(a, b, step, roll):
    low = (iota(a.shape, 1) & step) == 0
    return jnp.where(low, a, roll(b, step)), jnp.where(low, roll(a, 128 - step), b)


def lane_roll(x, by):
    return pltpu.roll(x, by, 1)


def kernel(state_hbm, gates_hbm, out, state, gates, s1, r1, s2, r2, s3, r3, s4, r4, m0, m1, m2, firsts, *sems):
    load, send1, recv1, send2, recv2, send3, recv3, send4, recv4, relay = sems
    wide = lax.axis_index("wide")
    narrow = lax.axis_index("narrow")
    z = narrow // 2
    rest = (narrow % 2) * 8 + wide % 8
    plane = (wide // 8) * 16 + rest

    def plane_id(p):
        return ((p // 16) * 8 + p % 8, z * 2 + (p // 8) % 2)

    def rest_id(p):
        return ((wide // 8) * 8 + p % 8, z * 2 + p // 8)

    def z_id(other):
        return (wide, other * 2 + narrow % 2)

    def z_slot(other):
        return (other % 4) * 8 + other // 4

    def signal_z(sem, step):
        for other in ((z + step) % NZ, (z + NZ - step) % NZ):
            pl.semaphore_signal(sem, inc=1, device_id=z_id(other), device_id_type=MESH)

    def relay_on(step):
        pl.semaphore_wait(relay.at[step], 2)
        if step < 3:
            signal_z(relay.at[step + 1], 2 << step)

    barrier = pltpu.get_barrier_semaphore()

    def greet(k, _):
        pl.semaphore_signal(barrier, inc=1, device_id=plane_id((plane + k) % NP), device_id_type=MESH)
        return 0

    signal_z(barrier, 1)
    lax.fori_loop(1, NP, greet, 0)
    loads = [
        pltpu.make_async_copy(gates_hbm.at[pl.ds(0, 2)], gates.at[pl.ds(0, 2)], load.at[0]),
        pltpu.make_async_copy(state_hbm, state, load.at[1]),
        pltpu.make_async_copy(gates_hbm.at[pl.ds(2, 4)], gates.at[pl.ds(2, 4)], load.at[2]),
    ]
    for copy in loads:
        copy.start()

    def exchange(source, target, own, peers, who, send, recv, h):
        def copy(p):
            return pltpu.make_async_remote_copy(
                src_ref=source(p),
                dst_ref=target,
                send_sem=send.at[h],
                recv_sem=recv.at[h],
                device_id=who(p),
                device_id_type=MESH,
            )

        pltpu.make_async_copy(source(own), target, recv.at[h]).start()

        def go(k, _):
            copy((own + k) % peers).start()
            return 0

        lax.fori_loop(1, peers, go, 0)

    def exchange_z(source, target, send, recv, h):
        def copy(p):
            return pltpu.make_async_remote_copy(
                src_ref=source.at[h, pl.ds(pl.multiple_of(p * 8, 8), 8)],
                dst_ref=target,
                send_sem=send.at[h],
                recv_sem=recv.at[h],
                device_id=z_id(p),
                device_id_type=MESH,
            )

        copy((z + 16) % NZ).start()

        def go(k, _):
            copy((z + 16 - k) % NZ).start()
            copy((z + 16 + k) % NZ).start()
            return 0

        lax.fori_loop(1, 16, go, 0)
        pltpu.make_async_copy(source.at[h, pl.ds(pl.multiple_of(z * 8, 8), 8)], target, recv.at[h]).start()

    def arrived(ref, sem):
        pltpu.make_async_copy(ref, ref, sem).wait()

    loads[0].wait()
    real, imag = select_second(gates[1], 0, 512)
    pl.semaphore_wait(barrier, 33)
    signal_z(relay.at[0], 1)
    m0[...] = join_second(real, imag, 0, 512)
    relay_on(0)
    loads[1].wait()
    loads[2].wait()
    both = first_gate([state[pl.ds(q, 128, 4), :] for q in range(4)], gates[0], 0, lane_roll)
    relay_on(1)
    for h in range(2):
        o = dot(both, m0[:, h * 256 : h * 256 + 256])
        for x in range(2):
            for p in range(8):
                a = o[p * 16 : p * 16 + 8, x * 128 : x * 128 + 128]
                b = o[p * 16 + 8 : p * 16 + 16, x * 128 : x * 128 + 128]
                s1[h, x * 16 + p], s1[h, x * 16 + 8 + p] = swap_half(a, b, 64, lane_roll)
        exchange(lambda p: s1.at[h, p], r1.at[h, plane], plane, NP, plane_id, send1, recv1, h)
    relay_on(2)
    relay_on(3)
    for h in range(2):
        arrived(r1.at[h], recv1.at[h])
        for p in range(8):
            v = [swap_half(r1[h, y * 8 + p], r1[h, 16 + y * 8 + p], 64, lane_roll) for y in range(2)]
            for c in range(2):
                pair = swap_half(v[0][c], v[1][c], 32, lane_roll)
                for b in range(2):
                    s2[h, pl.ds(c * 128 + b * 8 + p, 8, 16), :] = pair[b]
        exchange_z(s2, r2.at[h, z], send2, recv2, h)
    m1[...] = expand_second(gates[3], 1, 256)
    for t in range(2):
        firsts[t] = permute_first(gates[2 * t + 2])
    m2[...] = expand_second(gates[5], 2, 512)

    for h in range(2):
        arrived(r2.at[h], recv2.at[h])
        tiles = []
        for b in range(2):
            rows = []
            for k in range(8):
                rows += swap_half(r2[h, k * 4 + b], r2[h, k * 4 + 2 + b], 64, lane_roll)
            tiles.append(jnp.concatenate(rows, axis=0))
        o = dot(first_gate(tiles, firsts[0], 1, lane_roll), m1[...])
        for t in range(2):
            s3[h, t * 8 : t * 8 + 8] = o[:, t * 128 : t * 128 + 128].reshape(8, 16, 128)
        exchange(lambda p: s3.at[h, p], r3.at[h, rest], rest, 16, rest_id, send3, recv3, h)
        arrived(r3.at[h], recv3.at[h])
        for p in range(8):
            pair = swap_half(r3[h, p], r3[h, 8 + p], 64, lane_roll)
            for b in range(2):
                s4[h, pl.ds(b * 8 + p, 16, 16), :] = pair[b]
        exchange_z(s4, r4.at[h, z_slot(z)], send4, recv4, h)

    for h in range(2):
        arrived(r4.at[h], recv4.at[h])
    tiles = []
    for q in range(4):
        rows = []
        for k in range(8):
            rows += [r4[0, q * 8 + k], r4[1, q * 8 + k]]
        tiles.append(jnp.concatenate(rows, axis=0))
    o = dot(first_gate(tiles, firsts[1], 2, lane_roll), m2[...])
    for c in range(2):
        for s in range(2):
            q = c * 2 + s
            out[pl.ds(s * 256 + c, 128, 2), :] = o[:, q * 128 : q * 128 + 128]
    for h in range(2):
        for sent, sem in ((s1.at[h, pl.ds(0, 31)], send1), (r2.at[h, pl.ds(0, 31)], send2),
                          (s3.at[h, pl.ds(0, 15)], send3), (r4.at[h, pl.ds(0, 31)], send4)):
            pltpu.make_async_copy(sent, sent, sem.at[h]).wait()


def on_device(state, gates):
    rows = state.reshape(2, 256, 128).transpose(1, 0, 2).reshape(512, 128)
    hbm = pl.BlockSpec(memory_space=pl.ANY)
    out = pl.pallas_call(
        kernel,
        out_shape=pltpu.VMEM((512, 128), jnp.float32),
        in_specs=[hbm, hbm],
        out_specs=pl.BlockSpec(memory_space=pltpu.VMEM),
        scratch_shapes=[
            pltpu.VMEM((512, 128), jnp.float32),
            pltpu.VMEM((6, 256, 128), jnp.float32),
            pltpu.VMEM((2, NP, 8, 128), jnp.float32),
            pltpu.VMEM((2, NP, 8, 128), jnp.float32),
            pltpu.VMEM((2, NZ * 8, 128), jnp.float32),
            pltpu.VMEM((2, NZ, 8, 128), jnp.float32),
            pltpu.VMEM((2, 16, 16, 128), jnp.float32),
            pltpu.VMEM((2, 16, 16, 128), jnp.float32),
            pltpu.VMEM((2, NZ * 8, 128), jnp.float32),
            pltpu.VMEM((2, NZ, 8, 128), jnp.float32),
            pltpu.VMEM((512, 512), jnp.float32),
            pltpu.VMEM((256, 256), jnp.float32),
            pltpu.VMEM((512, 512), jnp.float32),
            pltpu.VMEM((2, 256, 128), jnp.float32),
            pltpu.SemaphoreType.DMA((3,)),
        ]
        + [pltpu.SemaphoreType.DMA((2,))] * 8
        + [pltpu.SemaphoreType.REGULAR((4,))],
        compiler_params=pltpu.CompilerParams(collective_id=0, has_side_effects=True),
        name="window",
    )(rows, gates.reshape(6, 256, 128))
    return out.reshape(256, 2, 128).transpose(1, 0, 2).reshape(2, 32768)


def solution(mesh):
    return jax.shard_map(
        on_device,
        mesh=mesh,
        in_specs=(P(None, AXES), P()),
        out_specs=P(None, AXES),
        check_vma=False,
    )
```

```python
import jax
import jax.numpy as jnp
from jax import lax
from jax.experimental import pallas as pl
from jax.experimental.pallas import tpu as pltpu
from jax.sharding import PartitionSpec as P

AXES = ("wide", "narrow")
MESH = pl.DeviceIdType.MESH
NZ = 32
NP = 32


def dot(a, b):
    return lax.dot_general(
        a, b, (((1,), (0,)), ((), ())), precision=lax.Precision.HIGHEST, preferred_element_type=jnp.float32
    )


def dot_nt(a, b):
    return lax.dot_general(
        a, b, (((1,), (1,)), ((), ())), precision=lax.Precision.HIGHEST, preferred_element_type=jnp.float32
    )


def iota(shape, dim):
    return lax.broadcasted_iota(jnp.int32, shape, dim)


def in_parts(k, l):
    if l == 1:
        return ((k >> 6) & 1) * 64 + (k >> 7) * 32 + ((k >> 5) & 1) * 16 + (k & 15), (k >> 4) & 1
    return ((k >> 4) & 1) * 64 + (k >> 7) * 32 + ((k >> 6) & 1) * 16 + (k & 15), (k >> 5) & 1


def out_parts(k, l):
    if l == 0:
        return ((k >> 5) & 1) * 64 + ((k >> 6) & 1) * 32 + (k & 15) * 2 + (k >> 7), (k >> 4) & 1
    if l == 1:
        return ((k >> 6) & 1) * 64 + (k >> 7) * 32 + (k & 15) * 2 + ((k >> 4) & 1), (k >> 5) & 1
    return k & 127, k >> 7


def expand_second(u, l):
    i2, _ = in_parts(iota((256, 128), 0), l)
    rows = (i2 == iota((256, 128), 1)).astype(jnp.float32)
    j2, _ = out_parts(iota((128, 256), 1), l)
    cols = (j2 == iota((128, 256), 0)).astype(jnp.float32)
    real, imag = (dot(dot_nt(rows, part), cols) for part in (u[:128], u[128:]))
    _, c_in = in_parts(iota((256, 256), 0), l)
    _, c_out = out_parts(iota((256, 256), 1), l)
    return jnp.where(c_in == c_out, real, jnp.where(c_in < c_out, imag, -imag))


def second_rows(u):
    j2, _ = out_parts(iota((256, 128), 0), 0)
    pick = (j2 == iota((256, 128), 1)).astype(jnp.float32)
    real, imag = dot(pick, u[:128]), dot(pick, u[128:])
    _, c_out = out_parts(iota((256, 128), 0), 0)
    return jnp.concatenate([jnp.where(c_out == 0, real, imag), jnp.where(c_out == 0, -imag, real)], axis=1)


def part_s(x):
    k = iota((256, 256), 0)
    pick = ((k & 1) * 128 + (k >> 1) == iota((256, 256), 1)).astype(jnp.float32).astype(jnp.bfloat16)
    high = x.astype(jnp.bfloat16)
    left = x - high.astype(jnp.float32)
    mid = left.astype(jnp.bfloat16)
    low = (left - mid.astype(jnp.float32)).astype(jnp.bfloat16)
    a, b, c = (jnp.dot(part, pick, preferred_element_type=jnp.float32) for part in (high, mid, low))
    return (a + b) + c


def layer_zero(tiles, u1, m):
    re, im = (part_s(jnp.concatenate([tiles[c], tiles[2 + c]], axis=1)) for c in range(2))
    re, im = dot(u1, re), dot(u1, im)
    z_re, z_im = re[:128] - im[128:], im[:128] + re[128:]
    return [
        dot_nt(jnp.concatenate([z_re[:, k * 128 : k * 128 + 128], z_im[:, k * 128 : k * 128 + 128]], axis=1), m)
        for k in range(2)
    ]


def permute_first(u):
    k = iota((128, 128), 1)
    pick = (iota((128, 128), 0) == (k & 15) * 8 + (k >> 4)).astype(jnp.float32)
    return dot(u, pick)


def times_i(tiles, l, roll):
    step = 16 if l == 1 else 32
    real = (iota((128, 128), 1) & step) == 0
    return [jnp.where(real, -roll(t, 128 - step), roll(t, step)) for t in tiles]


def first_gate(tiles, u1, l, roll):
    both = [dot(u1, t) for t in tiles]
    turned = times_i([t[128:] for t in both], l, roll)
    return [a[:128] + b for a, b in zip(both, turned)]


def swap_half(a, b, step, roll):
    low = (iota(a.shape, 1) & step) == 0
    return jnp.where(low, a, roll(b, step)), jnp.where(low, roll(a, 128 - step), b)


def lane_roll(x, by):
    return pltpu.roll(x, by, 1)


def kernel(state_hbm, gates_hbm, out, state, gates, s1, r1, s2, r2, s3, r3, s4, r4, m1, m2, firsts, *sems):
    load, send1, recv1, send2, recv2, send3, recv3, send4, recv4, relay = sems
    wide = lax.axis_index("wide")
    narrow = lax.axis_index("narrow")
    z = narrow // 2
    rest = (narrow % 2) * 8 + wide % 8
    plane = (wide // 8) * 16 + rest

    def plane_id(p):
        return ((p // 16) * 8 + p % 8, z * 2 + (p // 8) % 2)

    def rest_id(p):
        return ((wide // 8) * 8 + p % 8, z * 2 + p // 8)

    def z_id(other):
        return (wide, other * 2 + narrow % 2)

    def z_slot(other):
        return (other % 4) * 8 + other // 4

    def signal_z(sem, step):
        for other in ((z + step) % NZ, (z + NZ - step) % NZ):
            pl.semaphore_signal(sem, inc=1, device_id=z_id(other), device_id_type=MESH)

    def relay_on(step):
        pl.semaphore_wait(relay.at[step], 2)
        if step < 3:
            signal_z(relay.at[step + 1], 2 << step)

    barrier = pltpu.get_barrier_semaphore()

    def greet(k, _):
        pl.semaphore_signal(barrier, inc=1, device_id=plane_id((plane + k) % NP), device_id_type=MESH)
        return 0

    loads = [
        pltpu.make_async_copy(gates_hbm.at[pl.ds(0, 2)], gates.at[pl.ds(0, 2)], load.at[0]),
        pltpu.make_async_copy(state_hbm, state, load.at[1]),
        pltpu.make_async_copy(gates_hbm.at[pl.ds(2, 4)], gates.at[pl.ds(2, 4)], load.at[2]),
    ]
    for copy in loads:
        copy.start()

    signal_z(barrier, 1)
    lax.fori_loop(1, NP, greet, 0)
    def exchange(source, target, own, peers, who, send, recv, h):
        def copy(p):
            return pltpu.make_async_remote_copy(
                src_ref=source(p),
                dst_ref=target,
                send_sem=send.at[h],
                recv_sem=recv.at[h],
                device_id=who(p),
                device_id_type=MESH,
            )

        pltpu.make_async_copy(source(own), target, recv.at[h]).start()

        def go(k, _):
            copy((own + k) % peers).start()
            return 0

        lax.fori_loop(1, peers, go, 0)

    def exchange_z(source, target, send, recv, h, first=0, last=16):
        def copy(p):
            p = p % NZ
            return pltpu.make_async_remote_copy(
                src_ref=source.at[h, pl.ds(pl.multiple_of(p * 8, 8), 8)],
                dst_ref=target,
                send_sem=send.at[h],
                recv_sem=recv.at[h],
                device_id=z_id(p),
                device_id_type=MESH,
            )

        def go(k, _):
            copy(z + 16 - k).start()
            copy(z + 16 + k).start()
            return 0

        if first == 0:
            copy(z + 16).start()
        lax.fori_loop(max(first, 1), last, go, 0)
        if first > 0:
            return
        pltpu.make_async_copy(source.at[h, pl.ds(pl.multiple_of(z * 8, 8), 8)], target, recv.at[h]).start()

    def arrived(ref, sem):
        pltpu.make_async_copy(ref, ref, sem).wait()

    loads[0].wait()
    m0 = second_rows(gates[1])
    loads[1].wait()
    halves = layer_zero([state[pl.ds(q, 128, 4), :] for q in range(4)], gates[0], m0)
    for h in range(2):
        o = halves[h]
        for x in range(2):
            for p in range(8):
                a = o[p * 16 : p * 16 + 8, x * 128 : x * 128 + 128]
                b = o[p * 16 + 8 : p * 16 + 16, x * 128 : x * 128 + 128]
                s1[h, x * 16 + p], s1[h, x * 16 + 8 + p] = swap_half(a, b, 64, lane_roll)
    pl.semaphore_wait(barrier, 33)
    signal_z(relay.at[0], 1)
    for h in range(2):
        exchange(lambda p: s1.at[h, p], r1.at[h, plane], plane, NP, plane_id, send1, recv1, h)
        relay_on(h)
    relay_on(2)
    for h in range(2):
        arrived(r1.at[h], recv1.at[h])
        for p in range(8):
            v = [swap_half(r1[h, y * 8 + p], r1[h, 16 + y * 8 + p], 64, lane_roll) for y in range(2)]
            for c in range(2):
                pair = swap_half(v[0][c], v[1][c], 32, lane_roll)
                for b in range(2):
                    s2[h, pl.ds(c * 128 + b * 8 + p, 8, 16), :] = pair[b]
        if h == 0:
            exchange_z(s2, r2.at[h, z], send2, recv2, h, 8, 16)
            relay_on(3)
            exchange_z(s2, r2.at[h, z], send2, recv2, h, 0, 8)
        else:
            exchange_z(s2, r2.at[h, z], send2, recv2, h)
    loads[2].wait()
    m1[...] = expand_second(gates[3], 1)
    for t in range(2):
        firsts[t] = permute_first(gates[2 * t + 2])
    m2[...] = expand_second(gates[5], 2)

    for h in range(2):
        arrived(r2.at[h], recv2.at[h])
        tiles = []
        for b in range(2):
            rows = []
            for k in range(8):
                rows += swap_half(r2[h, k * 4 + b], r2[h, k * 4 + 2 + b], 64, lane_roll)
            tiles.append(jnp.concatenate(rows, axis=0))
        o = dot(jnp.concatenate(first_gate(tiles, firsts[0], 1, lane_roll), axis=1), m1[...])
        for t in range(2):
            s3[h, t * 8 : t * 8 + 8] = o[:, t * 128 : t * 128 + 128].reshape(8, 16, 128)
        exchange(lambda p: s3.at[h, p], r3.at[h, rest], rest, 16, rest_id, send3, recv3, h)
        arrived(r3.at[h], recv3.at[h])
        for p in range(8):
            pair = swap_half(r3[h, p], r3[h, 8 + p], 64, lane_roll)
            for b in range(2):
                s4[h, pl.ds(b * 8 + p, 16, 16), :] = pair[b]
        exchange_z(s4, r4.at[h, z_slot(z)], send4, recv4, h)

    for h in range(2):
        arrived(r4.at[h], recv4.at[h])
    tiles = []
    for q in range(4):
        rows = []
        for k in range(8):
            rows += [r4[0, q * 8 + k], r4[1, q * 8 + k]]
        tiles.append(jnp.concatenate(rows, axis=0))
    lows = [swap_half(tiles[k], tiles[k + 2], 16, lane_roll) for k in range(2)]
    y = first_gate([lows[0][0], lows[1][0], lows[0][1], lows[1][1]], firsts[1], 2, lane_roll)
    wide_y = jnp.concatenate([jnp.concatenate(y[:2], axis=1), jnp.concatenate(y[2:], axis=1)], axis=0)
    o = dot(wide_y, m2[...])
    for c in range(2):
        for k in range(2):
            out[pl.ds(k * 256 + c, 128, 2), :] = o[k * 128 : k * 128 + 128, c * 128 : c * 128 + 128]
    for h in range(2):
        for sent, sem in ((s1.at[h, pl.ds(0, 31)], send1), (r2.at[h, pl.ds(0, 31)], send2),
                          (s3.at[h, pl.ds(0, 15)], send3), (r4.at[h, pl.ds(0, 31)], send4)):
            pltpu.make_async_copy(sent, sent, sem.at[h]).wait()


def on_device(state, gates):
    rows = state.reshape(2, 256, 128).transpose(1, 0, 2).reshape(512, 128)
    hbm = pl.BlockSpec(memory_space=pl.ANY)
    out = pl.pallas_call(
        kernel,
        out_shape=pltpu.VMEM((512, 128), jnp.float32),
        in_specs=[hbm, hbm],
        out_specs=pl.BlockSpec(memory_space=pltpu.VMEM),
        scratch_shapes=[
            pltpu.VMEM((512, 128), jnp.float32),
            pltpu.VMEM((6, 256, 128), jnp.float32),
            pltpu.VMEM((2, NP, 8, 128), jnp.float32),
            pltpu.VMEM((2, NP, 8, 128), jnp.float32),
            pltpu.VMEM((2, NZ * 8, 128), jnp.float32),
            pltpu.VMEM((2, NZ, 8, 128), jnp.float32),
            pltpu.VMEM((2, 16, 16, 128), jnp.float32),
            pltpu.VMEM((2, 16, 16, 128), jnp.float32),
            pltpu.VMEM((2, NZ * 8, 128), jnp.float32),
            pltpu.VMEM((2, NZ, 8, 128), jnp.float32),
            pltpu.VMEM((256, 256), jnp.float32),
            pltpu.VMEM((256, 256), jnp.float32),
            pltpu.VMEM((2, 256, 128), jnp.float32),
            pltpu.SemaphoreType.DMA((3,)),
        ]
        + [pltpu.SemaphoreType.DMA((2,))] * 8
        + [pltpu.SemaphoreType.REGULAR((4,))],
        compiler_params=pltpu.CompilerParams(collective_id=0, has_side_effects=True),
        name="window",
    )(rows, gates.reshape(6, 256, 128))
    return out.reshape(256, 2, 128).transpose(1, 0, 2).reshape(2, 32768)


def solution(mesh):
    return jax.shard_map(
        on_device,
        mesh=mesh,
        in_specs=(P(None, AXES), P()),
        out_specs=P(None, AXES),
        check_vma=False,
    )
```

```python
import jax
import jax.numpy as jnp
from jax import lax
from jax.experimental import pallas as pl
from jax.experimental.pallas import tpu as pltpu
from jax.sharding import PartitionSpec as P

AXES = ("wide", "narrow")
MESH = pl.DeviceIdType.MESH
NZ = 32
NP = 32


def dot(a, b):
    return lax.dot_general(
        a, b, (((1,), (0,)), ((), ())), precision=lax.Precision.HIGHEST, preferred_element_type=jnp.float32
    )


def dot_nt(a, b):
    return lax.dot_general(
        a, b, (((1,), (1,)), ((), ())), precision=lax.Precision.HIGHEST, preferred_element_type=jnp.float32
    )


def iota(shape, dim):
    return lax.broadcasted_iota(jnp.int32, shape, dim)


def in_parts(k, l):
    if l == 1:
        return ((k >> 6) & 1) * 64 + (k >> 7) * 32 + ((k >> 5) & 1) * 16 + (k & 15), (k >> 4) & 1
    return ((k >> 4) & 1) * 64 + (k >> 7) * 32 + ((k >> 6) & 1) * 16 + (k & 15), (k >> 5) & 1


def out_parts(k, l):
    if l == 0:
        return ((k >> 5) & 1) * 64 + ((k >> 6) & 1) * 32 + (k & 15) * 2 + (k >> 7), (k >> 4) & 1
    if l == 1:
        return ((k >> 6) & 1) * 64 + (k >> 7) * 32 + (k & 15) * 2 + ((k >> 4) & 1), (k >> 5) & 1
    return k & 127, k >> 7


def expand_second(u, l):
    i2, _ = in_parts(iota((256, 128), 0), l)
    rows = (i2 == iota((256, 128), 1)).astype(jnp.float32)
    j2, _ = out_parts(iota((128, 256), 1), l)
    cols = (j2 == iota((128, 256), 0)).astype(jnp.float32)
    real, imag = (dot(dot_nt(rows, part), cols) for part in (u[:128], u[128:]))
    _, c_in = in_parts(iota((256, 256), 0), l)
    _, c_out = out_parts(iota((256, 256), 1), l)
    return jnp.where(c_in == c_out, real, jnp.where(c_in < c_out, imag, -imag))


def second_rows(u):
    j2, _ = out_parts(iota((256, 128), 0), 0)
    pick = (j2 == iota((256, 128), 1)).astype(jnp.float32)
    real, imag = dot(pick, u[:128]), dot(pick, u[128:])
    _, c_out = out_parts(iota((256, 128), 0), 0)
    return jnp.concatenate([jnp.where(c_out == 0, real, imag), jnp.where(c_out == 0, -imag, real)], axis=1)


def part_s(x):
    k = iota((256, 256), 0)
    pick = ((k & 1) * 128 + (k >> 1) == iota((256, 256), 1)).astype(jnp.float32).astype(jnp.bfloat16)
    high = x.astype(jnp.bfloat16)
    left = x - high.astype(jnp.float32)
    mid = left.astype(jnp.bfloat16)
    low = (left - mid.astype(jnp.float32)).astype(jnp.bfloat16)
    a, b, c = (jnp.dot(part, pick, preferred_element_type=jnp.float32) for part in (high, mid, low))
    return (a + b) + c


def layer_zero(tiles, u1, m):
    re, im = (part_s(jnp.concatenate([tiles[c], tiles[2 + c]], axis=1)) for c in range(2))
    re, im = dot(u1, re), dot(u1, im)
    z_re, z_im = re[:128] - im[128:], im[:128] + re[128:]
    return [
        dot_nt(jnp.concatenate([z_re[:, k * 128 : k * 128 + 128], z_im[:, k * 128 : k * 128 + 128]], axis=1), m)
        for k in range(2)
    ]


def permute_first(u):
    k = iota((128, 128), 1)
    pick = (iota((128, 128), 0) == (k & 15) * 8 + (k >> 4)).astype(jnp.float32)
    return dot(u, pick)


def times_i(tiles, l, roll):
    step = 16 if l == 1 else 32
    real = (iota((128, 128), 1) & step) == 0
    return [jnp.where(real, -roll(t, 128 - step), roll(t, step)) for t in tiles]


def first_gate(tiles, u1, l, roll):
    both = [dot(u1, t) for t in tiles]
    turned = times_i([t[128:] for t in both], l, roll)
    return [a[:128] + b for a, b in zip(both, turned)]


def swap_half(a, b, step, roll):
    low = (iota(a.shape, 1) & step) == 0
    return jnp.where(low, a, roll(b, step)), jnp.where(low, roll(a, 128 - step), b)


def lane_roll(x, by):
    return pltpu.roll(x, by, 1)


def kernel(state_hbm, gates_hbm, out, state, gates, s1, r1, s2, r2, s3, r3, s4, r4, m1, m2, firsts, *sems):
    load, send1, recv1, send2, recv2, send3, recv3, send4, recv4, relay = sems
    wide = lax.axis_index("wide")
    narrow = lax.axis_index("narrow")
    z = narrow // 2
    rest = (narrow % 2) * 8 + wide % 8
    plane = (wide // 8) * 16 + rest

    def plane_id(p):
        return ((p // 16) * 8 + p % 8, z * 2 + (p // 8) % 2)

    def rest_id(p):
        return ((wide // 8) * 8 + p % 8, z * 2 + p // 8)

    def z_id(other):
        return (wide, other * 2 + narrow % 2)

    def z_slot(other):
        return (other % 4) * 8 + other // 4

    def signal_z(sem, step):
        for other in ((z + step) % NZ, (z + NZ - step) % NZ):
            pl.semaphore_signal(sem, inc=1, device_id=z_id(other), device_id_type=MESH)

    def relay_on(step):
        pl.semaphore_wait(relay.at[step], 2)
        if step < 3:
            signal_z(relay.at[step + 1], 2 << step)

    barrier = pltpu.get_barrier_semaphore()

    def greet(k, _):
        pl.semaphore_signal(barrier, inc=1, device_id=plane_id((plane + k) % NP), device_id_type=MESH)
        return 0

    loads = [
        pltpu.make_async_copy(gates_hbm.at[pl.ds(0, 2)], gates.at[pl.ds(0, 2)], load.at[0]),
        pltpu.make_async_copy(state_hbm, state, load.at[1]),
        pltpu.make_async_copy(gates_hbm.at[pl.ds(2, 4)], gates.at[pl.ds(2, 4)], load.at[2]),
    ]
    for copy in loads:
        copy.start()

    signal_z(barrier, 1)
    lax.fori_loop(1, NP, greet, 0)
    def exchange(source, target, own, peers, who, send, recv, h):
        def copy(p):
            return pltpu.make_async_remote_copy(
                src_ref=source(p),
                dst_ref=target,
                send_sem=send.at[h],
                recv_sem=recv.at[h],
                device_id=who(p),
                device_id_type=MESH,
            )

        pltpu.make_async_copy(source(own), target, recv.at[h]).start()

        def go(k, _):
            copy((own + k) % peers).start()
            return 0

        lax.fori_loop(1, peers, go, 0)

    def exchange_z(source, target, send, recv, h, first=0, last=16):
        def copy(p):
            p = p % NZ
            return pltpu.make_async_remote_copy(
                src_ref=source.at[h, pl.ds(pl.multiple_of(p * 8, 8), 8)],
                dst_ref=target,
                send_sem=send.at[h],
                recv_sem=recv.at[h],
                device_id=z_id(p),
                device_id_type=MESH,
            )

        def go(k, _):
            copy(z + 16 - k).start()
            copy(z + 16 + k).start()
            return 0

        if first == 0:
            copy(z + 16).start()
        lax.fori_loop(max(first, 1), last, go, 0)
        if first > 0:
            return
        pltpu.make_async_copy(source.at[h, pl.ds(pl.multiple_of(z * 8, 8), 8)], target, recv.at[h]).start()

    def arrived(ref, sem):
        pltpu.make_async_copy(ref, ref, sem).wait()

    loads[0].wait()
    m0 = second_rows(gates[1])
    loads[1].wait()
    halves = layer_zero([state[pl.ds(q, 128, 4), :] for q in range(4)], gates[0], m0)
    for h in range(2):
        o = halves[h]
        for x in range(2):
            for p in range(8):
                a = o[p * 16 : p * 16 + 8, x * 128 : x * 128 + 128]
                b = o[p * 16 + 8 : p * 16 + 16, x * 128 : x * 128 + 128]
                s1[h, x * 16 + p], s1[h, x * 16 + 8 + p] = swap_half(a, b, 64, lane_roll)
    pl.semaphore_wait(barrier, 33)
    signal_z(relay.at[0], 1)
    for h in range(2):
        exchange(lambda p: s1.at[h, p], r1.at[h, plane], plane, NP, plane_id, send1, recv1, h)
        relay_on(h)
    relay_on(2)

    def pack(h):
        arrived(r1.at[h], recv1.at[h])
        for p in range(8):
            v = [swap_half(r1[h, y * 8 + p], r1[h, 16 + y * 8 + p], 64, lane_roll) for y in range(2)]
            for c in range(2):
                pair = swap_half(v[0][c], v[1][c], 32, lane_roll)
                for b in range(2):
                    s2[h, pl.ds(c * 128 + b * 8 + p, 8, 16), :] = pair[b]

    pack(0)
    exchange_z(s2, r2.at[0, z], send2, recv2, 0, 8, 12)
    pack(1)
    relay_on(3)
    exchange_z(s2, r2.at[0, z], send2, recv2, 0, 0, 8)
    exchange_z(s2, r2.at[0, z], send2, recv2, 0, 12, 16)
    exchange_z(s2, r2.at[1, z], send2, recv2, 1, 0, 16)
    loads[2].wait()
    m1[...] = expand_second(gates[3], 1)
    for t in range(2):
        firsts[t] = permute_first(gates[2 * t + 2])
    m2[...] = expand_second(gates[5], 2)

    for h in range(2):
        arrived(r2.at[h], recv2.at[h])
        tiles = []
        for b in range(2):
            rows = []
            for k in range(8):
                rows += swap_half(r2[h, k * 4 + b], r2[h, k * 4 + 2 + b], 64, lane_roll)
            tiles.append(jnp.concatenate(rows, axis=0))
        o = dot(jnp.concatenate(first_gate(tiles, firsts[0], 1, lane_roll), axis=1), m1[...])
        for t in range(2):
            s3[h, t * 8 : t * 8 + 8] = o[:, t * 128 : t * 128 + 128].reshape(8, 16, 128)
        exchange(lambda p: s3.at[h, p], r3.at[h, rest], rest, 16, rest_id, send3, recv3, h)
        arrived(r3.at[h], recv3.at[h])
        for p in range(8):
            pair = swap_half(r3[h, p], r3[h, 8 + p], 64, lane_roll)
            for b in range(2):
                s4[h, pl.ds(b * 8 + p, 16, 16), :] = pair[b]
        exchange_z(s4, r4.at[h, z_slot(z)], send4, recv4, h)

    for h in range(2):
        arrived(r4.at[h], recv4.at[h])
    tiles = []
    for q in range(4):
        rows = []
        for k in range(8):
            rows += [r4[0, q * 8 + k], r4[1, q * 8 + k]]
        tiles.append(jnp.concatenate(rows, axis=0))
    lows = [swap_half(tiles[k], tiles[k + 2], 16, lane_roll) for k in range(2)]
    y = first_gate([lows[0][0], lows[1][0], lows[0][1], lows[1][1]], firsts[1], 2, lane_roll)
    wide_y = jnp.concatenate([jnp.concatenate(y[:2], axis=1), jnp.concatenate(y[2:], axis=1)], axis=0)
    o = dot(wide_y, m2[...])
    for c in range(2):
        for k in range(2):
            out[pl.ds(k * 256 + c, 128, 2), :] = o[k * 128 : k * 128 + 128, c * 128 : c * 128 + 128]
    for h in range(2):
        for sent, sem in ((s1.at[h, pl.ds(0, 31)], send1), (r2.at[h, pl.ds(0, 31)], send2),
                          (s3.at[h, pl.ds(0, 15)], send3), (r4.at[h, pl.ds(0, 31)], send4)):
            pltpu.make_async_copy(sent, sent, sem.at[h]).wait()


def on_device(state, gates):
    rows = state.reshape(2, 256, 128).transpose(1, 0, 2).reshape(512, 128)
    hbm = pl.BlockSpec(memory_space=pl.ANY)
    out = pl.pallas_call(
        kernel,
        out_shape=pltpu.VMEM((512, 128), jnp.float32),
        in_specs=[hbm, hbm],
        out_specs=pl.BlockSpec(memory_space=pltpu.VMEM),
        scratch_shapes=[
            pltpu.VMEM((512, 128), jnp.float32),
            pltpu.VMEM((6, 256, 128), jnp.float32),
            pltpu.VMEM((2, NP, 8, 128), jnp.float32),
            pltpu.VMEM((2, NP, 8, 128), jnp.float32),
            pltpu.VMEM((2, NZ * 8, 128), jnp.float32),
            pltpu.VMEM((2, NZ, 8, 128), jnp.float32),
            pltpu.VMEM((2, 16, 16, 128), jnp.float32),
            pltpu.VMEM((2, 16, 16, 128), jnp.float32),
            pltpu.VMEM((2, NZ * 8, 128), jnp.float32),
            pltpu.VMEM((2, NZ, 8, 128), jnp.float32),
            pltpu.VMEM((256, 256), jnp.float32),
            pltpu.VMEM((256, 256), jnp.float32),
            pltpu.VMEM((2, 256, 128), jnp.float32),
            pltpu.SemaphoreType.DMA((3,)),
        ]
        + [pltpu.SemaphoreType.DMA((2,))] * 8
        + [pltpu.SemaphoreType.REGULAR((4,))],
        compiler_params=pltpu.CompilerParams(collective_id=0, has_side_effects=True),
        name="window",
    )(rows, gates.reshape(6, 256, 128))
    return out.reshape(256, 2, 128).transpose(1, 0, 2).reshape(2, 32768)


def solution(mesh):
    return jax.shard_map(
        on_device,
        mesh=mesh,
        in_specs=(P(None, AXES), P()),
        out_specs=P(None, AXES),
        check_vma=False,
    )
```

```python
import jax
import jax.numpy as jnp
from jax import lax
from jax.experimental import pallas as pl
from jax.experimental.pallas import tpu as pltpu
from jax.sharding import PartitionSpec as P

AXES = ("wide", "narrow")
MESH = pl.DeviceIdType.MESH
NZ = 32
NP = 32


def dot(a, b):
    return lax.dot_general(
        a, b, (((1,), (0,)), ((), ())), precision=lax.Precision.HIGHEST, preferred_element_type=jnp.float32
    )


def dot_nt(a, b):
    return lax.dot_general(
        a, b, (((1,), (1,)), ((), ())), precision=lax.Precision.HIGHEST, preferred_element_type=jnp.float32
    )


def two_parts(x):
    high = x.astype(jnp.bfloat16)
    return high, (x - high.astype(jnp.float32)).astype(jnp.bfloat16)


def dot3(a, b, dims=((1,), (0,))):
    (ah, al), (bh, bl) = two_parts(a), two_parts(b)
    one = lambda p, q: lax.dot_general(p, q, (dims, ((), ())), preferred_element_type=jnp.float32)
    return one(ah, bh) + (one(ah, bl) + one(al, bh))


def iota(shape, dim):
    return lax.broadcasted_iota(jnp.int32, shape, dim)


def in_parts(k, l):
    if l == 1:
        return ((k >> 6) & 1) * 64 + (k >> 7) * 32 + ((k >> 5) & 1) * 16 + (k & 15), (k >> 4) & 1
    return ((k >> 4) & 1) * 64 + (k >> 7) * 32 + ((k >> 6) & 1) * 16 + (k & 15), (k >> 5) & 1


def out_parts(k, l):
    if l == 0:
        return ((k >> 5) & 1) * 64 + ((k >> 6) & 1) * 32 + (k & 15) * 2 + (k >> 7), (k >> 4) & 1
    if l == 1:
        return ((k >> 6) & 1) * 64 + (k >> 7) * 32 + (k & 15) * 2 + ((k >> 4) & 1), (k >> 5) & 1
    return k & 127, k >> 7


def expand_second(u, l):
    i2, _ = in_parts(iota((256, 128), 0), l)
    rows = (i2 == iota((256, 128), 1)).astype(jnp.float32)
    j2, _ = out_parts(iota((128, 256), 1), l)
    cols = (j2 == iota((128, 256), 0)).astype(jnp.float32)
    real, imag = (dot(dot_nt(rows, part), cols) for part in (u[:128], u[128:]))
    _, c_in = in_parts(iota((256, 256), 0), l)
    _, c_out = out_parts(iota((256, 256), 1), l)
    return jnp.where(c_in == c_out, real, jnp.where(c_in < c_out, imag, -imag))


def second_rows(u):
    j2, _ = out_parts(iota((256, 128), 0), 0)
    pick = (j2 == iota((256, 128), 1)).astype(jnp.float32)
    real, imag = dot(pick, u[:128]), dot(pick, u[128:])
    _, c_out = out_parts(iota((256, 128), 0), 0)
    return jnp.concatenate([jnp.where(c_out == 0, real, imag), jnp.where(c_out == 0, -imag, real)], axis=1)


def part_s(x):
    k = iota((256, 256), 0)
    pick = ((k & 1) * 128 + (k >> 1) == iota((256, 256), 1)).astype(jnp.float32).astype(jnp.bfloat16)
    high = x.astype(jnp.bfloat16)
    left = x - high.astype(jnp.float32)
    mid = left.astype(jnp.bfloat16)
    low = (left - mid.astype(jnp.float32)).astype(jnp.bfloat16)
    a, b, c = (jnp.dot(part, pick, preferred_element_type=jnp.float32) for part in (high, mid, low))
    return (a + b) + c


def layer_zero(tiles, u1, m):
    re, im = (part_s(jnp.concatenate([tiles[c], tiles[2 + c]], axis=1)) for c in range(2))
    re, im = dot3(u1, re), dot3(u1, im)
    z_re, z_im = re[:128] - im[128:], im[:128] + re[128:]
    return [
        dot3(jnp.concatenate([z_re[:, k * 128 : k * 128 + 128], z_im[:, k * 128 : k * 128 + 128]], axis=1), m, ((1,), (1,)))
        for k in range(2)
    ]


def permute_first(u):
    k = iota((128, 128), 1)
    pick = (iota((128, 128), 0) == (k & 15) * 8 + (k >> 4)).astype(jnp.float32)
    return dot(u, pick)


def times_i(tiles, l, roll):
    step = 16 if l == 1 else 32
    real = (iota((128, 128), 1) & step) == 0
    return [jnp.where(real, -roll(t, 128 - step), roll(t, step)) for t in tiles]


def first_gate(tiles, u1, l, roll):
    both = [dot3(u1, t) for t in tiles]
    turned = times_i([t[128:] for t in both], l, roll)
    return [a[:128] + b for a, b in zip(both, turned)]


def swap_half(a, b, step, roll):
    low = (iota(a.shape, 1) & step) == 0
    return jnp.where(low, a, roll(b, step)), jnp.where(low, roll(a, 128 - step), b)


def lane_roll(x, by):
    return pltpu.roll(x, by, 1)


def kernel(state_hbm, gates_hbm, out, state, gates, s1, r1, s2, r2, s3, r3, s4, r4, m1, m2, firsts, *sems):
    load, send1, recv1, send2, recv2, send3, recv3, send4, recv4, relay = sems
    wide = lax.axis_index("wide")
    narrow = lax.axis_index("narrow")
    z = narrow // 2
    rest = (narrow % 2) * 8 + wide % 8
    plane = (wide // 8) * 16 + rest

    def plane_id(p):
        return ((p // 16) * 8 + p % 8, z * 2 + (p // 8) % 2)

    def rest_id(p):
        return ((wide // 8) * 8 + p % 8, z * 2 + p // 8)

    def z_id(other):
        return (wide, other * 2 + narrow % 2)

    def z_slot(other):
        return (other % 4) * 8 + other // 4

    def signal_z(sem, step):
        for other in ((z + step) % NZ, (z + NZ - step) % NZ):
            pl.semaphore_signal(sem, inc=1, device_id=z_id(other), device_id_type=MESH)

    def relay_on(step):
        pl.semaphore_wait(relay.at[step], 2)
        if step < 3:
            signal_z(relay.at[step + 1], 2 << step)

    barrier = pltpu.get_barrier_semaphore()

    def greet(k, _):
        pl.semaphore_signal(barrier, inc=1, device_id=plane_id((plane + k) % NP), device_id_type=MESH)
        return 0

    loads = [
        pltpu.make_async_copy(gates_hbm.at[pl.ds(0, 2)], gates.at[pl.ds(0, 2)], load.at[0]),
        pltpu.make_async_copy(state_hbm, state, load.at[1]),
        pltpu.make_async_copy(gates_hbm.at[pl.ds(2, 4)], gates.at[pl.ds(2, 4)], load.at[2]),
    ]
    for copy in loads:
        copy.start()

    signal_z(barrier, 1)
    lax.fori_loop(1, NP, greet, 0)
    def exchange(source, target, own, peers, who, send, recv, h):
        def copy(p):
            return pltpu.make_async_remote_copy(
                src_ref=source(p),
                dst_ref=target,
                send_sem=send.at[h],
                recv_sem=recv.at[h],
                device_id=who(p),
                device_id_type=MESH,
            )

        pltpu.make_async_copy(source(own), target, recv.at[h]).start()

        def go(k, _):
            copy((own + k) % peers).start()
            return 0

        lax.fori_loop(1, peers, go, 0)

    def exchange_z(source, target, send, recv, h, first=0, last=16):
        def copy(p):
            p = p % NZ
            return pltpu.make_async_remote_copy(
                src_ref=source.at[h, pl.ds(pl.multiple_of(p * 8, 8), 8)],
                dst_ref=target,
                send_sem=send.at[h],
                recv_sem=recv.at[h],
                device_id=z_id(p),
                device_id_type=MESH,
            )

        def go(k, _):
            copy(z + 16 - k).start()
            copy(z + 16 + k).start()
            return 0

        if first == 0:
            copy(z + 16).start()
        lax.fori_loop(max(first, 1), last, go, 0)
        if first > 0:
            return
        pltpu.make_async_copy(source.at[h, pl.ds(pl.multiple_of(z * 8, 8), 8)], target, recv.at[h]).start()

    def arrived(ref, sem):
        pltpu.make_async_copy(ref, ref, sem).wait()

    loads[0].wait()
    m0 = second_rows(gates[1])
    loads[1].wait()
    halves = layer_zero([state[pl.ds(q, 128, 4), :] for q in range(4)], gates[0], m0)
    for h in range(2):
        o = halves[h]
        for x in range(2):
            for p in range(8):
                a = o[p * 16 : p * 16 + 8, x * 128 : x * 128 + 128]
                b = o[p * 16 + 8 : p * 16 + 16, x * 128 : x * 128 + 128]
                s1[h, x * 16 + p], s1[h, x * 16 + 8 + p] = swap_half(a, b, 64, lane_roll)
    pl.semaphore_wait(barrier, 33)
    signal_z(relay.at[0], 1)
    for h in range(2):
        exchange(lambda p: s1.at[h, p], r1.at[h, plane], plane, NP, plane_id, send1, recv1, h)
        relay_on(h)
    relay_on(2)

    def pack(h):
        arrived(r1.at[h], recv1.at[h])
        for p in range(8):
            v = [swap_half(r1[h, y * 8 + p], r1[h, 16 + y * 8 + p], 64, lane_roll) for y in range(2)]
            for c in range(2):
                pair = swap_half(v[0][c], v[1][c], 32, lane_roll)
                for b in range(2):
                    s2[h, pl.ds(c * 128 + b * 8 + p, 8, 16), :] = pair[b]

    pack(0)
    exchange_z(s2, r2.at[0, z], send2, recv2, 0, 8, 12)
    pack(1)
    relay_on(3)
    exchange_z(s2, r2.at[0, z], send2, recv2, 0, 0, 8)
    exchange_z(s2, r2.at[0, z], send2, recv2, 0, 12, 16)
    exchange_z(s2, r2.at[1, z], send2, recv2, 1, 0, 16)
    loads[2].wait()
    m1[...] = expand_second(gates[3], 1)
    for t in range(2):
        firsts[t] = permute_first(gates[2 * t + 2])
    m2[...] = expand_second(gates[5], 2)

    for h in range(2):
        arrived(r2.at[h], recv2.at[h])
        tiles = []
        for b in range(2):
            rows = []
            for k in range(8):
                rows += swap_half(r2[h, k * 4 + b], r2[h, k * 4 + 2 + b], 64, lane_roll)
            tiles.append(jnp.concatenate(rows, axis=0))
        o = dot3(jnp.concatenate(first_gate(tiles, firsts[0], 1, lane_roll), axis=1), m1[...])
        for t in range(2):
            s3[h, t * 8 : t * 8 + 8] = o[:, t * 128 : t * 128 + 128].reshape(8, 16, 128)
        exchange(lambda p: s3.at[h, p], r3.at[h, rest], rest, 16, rest_id, send3, recv3, h)
        arrived(r3.at[h], recv3.at[h])
        for p in range(8):
            pair = swap_half(r3[h, p], r3[h, 8 + p], 64, lane_roll)
            for b in range(2):
                s4[h, pl.ds(b * 8 + p, 16, 16), :] = pair[b]
        exchange_z(s4, r4.at[h, z_slot(z)], send4, recv4, h)

    for h in range(2):
        arrived(r4.at[h], recv4.at[h])
    tiles = []
    for q in range(4):
        rows = []
        for k in range(8):
            rows += [r4[0, q * 8 + k], r4[1, q * 8 + k]]
        tiles.append(jnp.concatenate(rows, axis=0))
    lows = [swap_half(tiles[k], tiles[k + 2], 16, lane_roll) for k in range(2)]
    y = first_gate([lows[0][0], lows[1][0], lows[0][1], lows[1][1]], firsts[1], 2, lane_roll)
    wide_y = jnp.concatenate([jnp.concatenate(y[:2], axis=1), jnp.concatenate(y[2:], axis=1)], axis=0)
    o = dot3(wide_y, m2[...])
    for c in range(2):
        for k in range(2):
            out[pl.ds(k * 256 + c, 128, 2), :] = o[k * 128 : k * 128 + 128, c * 128 : c * 128 + 128]
    for h in range(2):
        for sent, sem in ((s1.at[h, pl.ds(0, 31)], send1), (r2.at[h, pl.ds(0, 31)], send2),
                          (s3.at[h, pl.ds(0, 15)], send3), (r4.at[h, pl.ds(0, 31)], send4)):
            pltpu.make_async_copy(sent, sent, sem.at[h]).wait()


def on_device(state, gates):
    rows = state.reshape(2, 256, 128).transpose(1, 0, 2).reshape(512, 128)
    hbm = pl.BlockSpec(memory_space=pl.ANY)
    out = pl.pallas_call(
        kernel,
        out_shape=pltpu.VMEM((512, 128), jnp.float32),
        in_specs=[hbm, hbm],
        out_specs=pl.BlockSpec(memory_space=pltpu.VMEM),
        scratch_shapes=[
            pltpu.VMEM((512, 128), jnp.float32),
            pltpu.VMEM((6, 256, 128), jnp.float32),
            pltpu.VMEM((2, NP, 8, 128), jnp.float32),
            pltpu.VMEM((2, NP, 8, 128), jnp.float32),
            pltpu.VMEM((2, NZ * 8, 128), jnp.float32),
            pltpu.VMEM((2, NZ, 8, 128), jnp.float32),
            pltpu.VMEM((2, 16, 16, 128), jnp.float32),
            pltpu.VMEM((2, 16, 16, 128), jnp.float32),
            pltpu.VMEM((2, NZ * 8, 128), jnp.float32),
            pltpu.VMEM((2, NZ, 8, 128), jnp.float32),
            pltpu.VMEM((256, 256), jnp.float32),
            pltpu.VMEM((256, 256), jnp.float32),
            pltpu.VMEM((2, 256, 128), jnp.float32),
            pltpu.SemaphoreType.DMA((3,)),
        ]
        + [pltpu.SemaphoreType.DMA((2,))] * 8
        + [pltpu.SemaphoreType.REGULAR((4,))],
        compiler_params=pltpu.CompilerParams(collective_id=0, has_side_effects=True),
        name="window",
    )(rows, gates.reshape(6, 256, 128))
    return out.reshape(256, 2, 128).transpose(1, 0, 2).reshape(2, 32768)


def solution(mesh):
    return jax.shard_map(
        on_device,
        mesh=mesh,
        in_specs=(P(None, AXES), P()),
        out_specs=P(None, AXES),
        check_vma=False,
    )
```
